32 devices in a mesh: groups: 2 (over y), ctx: 4 (over z), head: 4 (over x, core).
Axes of the slice: x: 2, y: 2, z: 4, core: 2. Of those that a mesh axis runs over, the one named last changes fastest.
Arguments:
- queries: bfloat16 [8192, 2048], P(('groups', 'ctx'), 'head'), parts along dimension 0, may hold values from -6 to 6
- keys: bfloat16 [8192, 2048], P(('groups', 'ctx'), 'head'), parts along dimension 0, may hold values from -6 to 6
- values: bfloat16 [8192, 2048], P(('groups', 'ctx'), 'head'), parts along dimension 0, may hold values from -6 to 6
- offsets: int32 [3, 16], replicated, may hold values from 0 to 3, as said below
- w_out: bfloat16 [2048, 2048], P('head'), may hold values from -0.75 to 0.75
Outputs:
- mixed: bfloat16 [8192, 2048], P(('groups', 'ctx'), 'head'), parts along dimension 0
The draws below stay inside these ranges and needn't reach their ends.
There are 2 independent parts, one for each index of `groups`. The reference program is written for one: setup_inputs(seed, part) draws one part's arguments, and reference() takes and returns one part's arrays. A program takes and returns all parts, laid end to end along the dimension named above; an argument that names none is the same for every part. Nothing has to cross between parts.
Inputs may be any that keep to these rules, and one draw needn't show every extreme that they name: offsets[l, h] lies between 0 and 2**l - 1.
All inputs are finite; a program needn't handle non-finite values.
Results may differ from the reference program's by a relative error of at most 0.014.
Values may be sent and summed in bfloat16 or wider, within the bound.
No kernel may reach another device: no remote copies, remote signals or barrier semaphores. Data moves between devices by JAX's collectives and lax.ppermute only.
A program may use at most 64 MiB of HBM per device.

```python
import jax
import jax.numpy as jnp
from jax import lax

D = 2048
HEADS = 16
HD = 128
TOK_DEV = 1024
TOKENS = 4096
LEVELS = 3
GROUP_HEADS = 4
N_CTX = 4
N_HEAD = 4


def drawn_pair(key):
    base = jax.random.fold_in(key, 101)
    key_q, key_k = jax.random.split(base, 2)
    shape = (TOKENS, HEADS * HD)
    first = jnp.clip(1.5 * jax.random.normal(key_q, shape, jnp.float32), -6.0, 6.0)
    second = jnp.clip(jax.random.normal(key_k, shape, jnp.float32), -6.0, 6.0)
    return (first, second)


def draw_queries(key, part):
    return drawn_pair(key)[0].astype(jnp.bfloat16)


def draw_keys(key, part):
    return drawn_pair(key)[1].astype(jnp.bfloat16)


def draw_offsets(key, part):
    spans = jnp.left_shift(jnp.int32(1), jnp.arange(LEVELS, dtype=jnp.int32))
    raw = jax.random.randint(jax.random.fold_in(key, 3), (LEVELS, HEADS), 0, 1 << 30, dtype=jnp.int32) % spans[:, None]
    chosen = jax.random.randint(jax.random.fold_in(key, 7), (LEVELS,), 0, HEADS, dtype=jnp.int32)
    planted = jnp.arange(HEADS, dtype=jnp.int32)[None, :] == chosen[:, None]
    return jnp.where(planted, spans[:, None] - 1, raw)


def spiked(drawn, own_key, source, target, parts, factor):
    owner, partner = [(jnp.arange(drawn.shape[position]) // (drawn.shape[position] // parts)).reshape([-1 if axis == position else 1 for axis in range(drawn.ndim)]) for position in (source, target)]
    chosen = jax.random.permutation(own_key, parts)[partner]
    strong = (owner == chosen) | (owner == (partner + parts // 2) % parts)
    return jnp.where(strong, factor * drawn, drawn)


def steps_of(key, shape, pieces, low, top_value):
    def one(dim, parts):
        draws = jax.random.uniform(jax.random.fold_in(jax.random.fold_in(key, 6), dim), (parts,), jnp.float32, low / len(pieces), top_value / len(pieces))
        return jnp.repeat(jnp.exp(draws), shape[dim] // parts).reshape((-1,) + (1,) * (len(shape) - dim - 1))

    level = one(*pieces[0])
    for cut in pieces[1:]:
        level = level * one(*cut)
    return level


def centred(rng, dims, spread, most, pieces=(), held_as=jnp.bfloat16):
    result = spread * jax.random.normal(rng, dims, jnp.float32)
    if pieces:
        result = result * steps_of(rng, dims, pieces, -0.22, 0.18)
    return jnp.clip(result, -most, most).astype(held_as)


def bell_draw_with(stream_key, extent, scale, bound, pieces, heavy, kind=jnp.bfloat16):
    values = scale * jax.random.normal(stream_key, extent, jnp.float32)
    if pieces:
        values = values * steps_of(stream_key, extent, pieces, -0.22, 0.18)
    return jnp.clip(spiked(values, jax.random.fold_in(stream_key, 3), *heavy), -bound, bound).astype(kind)


def setup_inputs(seed: int = 0, part: int = 0) -> dict:
    key_of = jax.random.split(jax.random.key(seed), 6)
    part_splits = jax.random.split(jax.random.fold_in(key_of[5], part), 6)
    return {
        "queries": draw_queries(jax.random.fold_in(jax.random.fold_in(key_of[5], part), 71), part),
        "keys": draw_keys(jax.random.fold_in(jax.random.fold_in(key_of[5], part), 71), part),
        "values": centred(part_splits[2], (TOKENS, HEADS * HD), 1.0, 6.0, ((0, 4), (1, 4))),
        "offsets": draw_offsets(jax.random.fold_in(key_of[5], 71), part),
        "w_out": bell_draw_with(key_of[4], (HEADS * HD, D), HD ** -0.5, 0.75, ((0, 4),), (0, 1, 4, 2.0)),
    }


def one_level(qs, ks, vs, scale):
    scores = jnp.einsum("sqd,skd->sqk", qs.astype(jnp.float32), ks.astype(jnp.float32), precision=lax.Precision.HIGHEST) * scale
    top = jnp.max(scores, axis=-1, keepdims=True)
    expo = jnp.exp(scores - top)
    den = jnp.sum(expo, axis=-1)
    probs = expo.astype(jnp.bfloat16)
    out = jnp.einsum("sqk,skd->sqd", probs.astype(jnp.float32), vs.astype(jnp.float32), precision=lax.Precision.HIGHEST) / den[..., None]
    return out, top[..., 0] + jnp.log(den)


def reference(queries, keys, values, offsets, w_out):
    tokens = queries.shape[0]
    scale = HD ** -0.5

    def split_heads(block):
        return block.reshape(tokens, HEADS, HD).transpose(1, 0, 2)

    def one_head(item):
        q_head, k_head, v_head, phase = item
        best = None
        total = None
        acc = None
        for level in range(LEVELS):
            stride = 2 ** level
            segs = N_CTX // stride
            hit = jnp.arange(stride, dtype=jnp.int32) == phase[level]

            def pick(block):
                shaped = block.reshape(tokens // stride, stride, HD)
                return lax.dynamic_index_in_dim(shaped, phase[level], axis=1, keepdims=False).reshape(segs, TOK_DEV, HD)

            out, lse = one_level(pick(q_head), pick(k_head), pick(v_head), scale)
            out = out.reshape(tokens // stride, 1, HD)
            lse = lse.reshape(tokens // stride, 1)
            full_out = jnp.where(hit[None, :, None], out, jnp.float32(0.0)).reshape(tokens, HD)
            mask = jnp.broadcast_to(hit[None, :], (tokens // stride, stride)).reshape(tokens)
            full_lse = jnp.broadcast_to(lse, (tokens // stride, stride)).reshape(tokens)
            if level == 0:
                best = full_lse
                total = jnp.ones_like(full_lse)
                acc = full_out
            else:
                cand = jnp.where(mask, full_lse, best)
                newbest = jnp.maximum(best, cand)
                carry = jnp.exp(best - newbest)
                weight = jnp.where(mask, jnp.exp(cand - newbest), jnp.float32(0.0))
                total = total * carry + weight
                acc = acc * carry[:, None] + weight[:, None] * full_out
                best = newbest
        return acc / total[:, None]

    attn = lax.map(one_head, (split_heads(queries), split_heads(keys), split_heads(values), offsets.T))
    attn = attn.transpose(1, 0, 2).reshape(tokens, HEADS * HD).astype(jnp.bfloat16)
    width = GROUP_HEADS * HD
    summed = jnp.zeros((tokens, D), jnp.float32)
    for group in range(N_HEAD):
        term = jnp.dot(attn[:, group * width:(group + 1) * width], w_out[group * width:(group + 1) * width, :], preferred_element_type=jnp.float32)
        rounded = lax.optimization_barrier(term.astype(jnp.bfloat16))
        summed = summed + rounded.astype(jnp.float32)
    return summed.astype(jnp.bfloat16)
```

```python
import jax
import jax.numpy as jnp
from jax import lax
from jax.experimental import pallas as pl
from jax.experimental.pallas import tpu as pltpu
from jax.sharding import PartitionSpec as P

HD = 128


def swapped(shard, axis, stride):
    return lax.ppermute(shard, axis, [(i, i ^ 1 << stride) for i in range(lax.axis_size(axis))])


def select_rows(block, onehot):
    stride = onehot.shape[1]
    shaped = block.reshape(block.shape[0] // stride, stride, block.shape[1], block.shape[2])
    return jnp.einsum("nrhd,hr->hnd", shaped, onehot, preferred_element_type=jnp.float32).astype(
        jnp.bfloat16
    )


def attend(q_sel, k_all, v_all, scale):
    scores = jnp.einsum("hqd,hkd->hqk", q_sel, k_all, preferred_element_type=jnp.float32) * scale
    top = jnp.max(scores, axis=-1, keepdims=True)
    expo = jnp.exp(scores - top)
    den = jnp.sum(expo, axis=-1)
    probs = expo.astype(jnp.bfloat16)
    out = (
        jnp.einsum("hqk,hkd->hqd", probs, v_all, preferred_element_type=jnp.float32)
        / den[..., None]
    )
    return (out, top[..., 0] + jnp.log(den))


def shards(queries, keys, values, offsets, w_out):
    rows = queries.shape[0]
    local_heads = queries.shape[1] // HD
    levels = lax.axis_size("ctx").bit_length()
    scale = HD ** (-0.5)
    q_three = queries.reshape(rows, local_heads, HD)
    k_three = keys.reshape(rows, local_heads, HD)
    v_three = values.reshape(rows, local_heads, HD)
    first_head = lax.axis_index("head") * local_heads
    hits = []
    q_sels = []
    k_sels = []
    v_sels = []
    for level in range(levels):
        stride = 2**level
        phase = lax.dynamic_slice_in_dim(offsets[level], first_head, local_heads)
        hit = lax.broadcasted_iota(jnp.int32, (local_heads, stride), 1) == phase[:, None]
        onehot = hit.astype(jnp.bfloat16)
        hits.append(hit)
        q_sels.append(select_rows(q_three, onehot))
        k_sels.append(select_rows(k_three, onehot))
        v_sels.append(select_rows(v_three, onehot))
    for bit in range(levels - 1):
        active = list(range(bit + 1, levels))
        counts = [k_sels[level].shape[1] for level in active]
        joint_k = jnp.concatenate([k_sels[level] for level in active], axis=1)
        joint_v = jnp.concatenate([v_sels[level] for level in active], axis=1)
        recv_k, recv_v = swapped((joint_k, joint_v), "ctx", bit)
        start = 0
        for level, count in zip(active, counts):
            k_sels[level] = jnp.concatenate(
                [k_sels[level], recv_k[:, start : start + count]], axis=1
            )
            v_sels[level] = jnp.concatenate(
                [v_sels[level], recv_v[:, start : start + count]], axis=1
            )
            start = start + count
    best = None
    total = None
    acc = None
    for level in range(levels):
        stride = 2**level
        count = rows // stride
        out, lse = attend(q_sels[level], k_sels[level], v_sels[level], scale)
        hit = hits[level]
        full_out = (out[:, :, None, :] * hit[:, None, :, None].astype(jnp.float32)).reshape(
            local_heads, rows, HD
        )
        mask = jnp.broadcast_to(hit[:, None, :], (local_heads, count, stride)).reshape(
            local_heads, rows
        )
        full_lse = jnp.broadcast_to(lse[:, :, None], (local_heads, count, stride)).reshape(
            local_heads, rows
        )
        if level == 0:
            best = full_lse
            total = jnp.ones_like(full_lse)
            acc = full_out
        else:
            cand = jnp.where(mask, full_lse, best)
            newbest = jnp.maximum(best, cand)
            carry = jnp.exp(best - newbest)
            weight = jnp.where(mask, jnp.exp(cand - newbest), jnp.float32(0.0))
            total = total * carry + weight
            acc = acc * carry[..., None] + weight[..., None] * full_out
            best = newbest
    attn = (
        (acc / total[..., None])
        .transpose(1, 0, 2)
        .reshape(rows, local_heads * HD)
        .astype(jnp.bfloat16)
    )
    partial_value = jnp.dot(attn, w_out, preferred_element_type=jnp.float32)
    summed = lax.psum_scatter(
        partial_value.astype(jnp.bfloat16), "head", scatter_dimension=1, tiled=True
    )
    return summed


LOG2E = 1.4426950408889634
STAT = 16
NEG = -1e30


def dot_nt(a, b):
    return lax.dot_general(a, b, (((1,), (1,)), ((), ())), preferred_element_type=jnp.float32)


def dot_nn(a, b):
    return jnp.dot(a, b, preferred_element_type=jnp.float32)


def stack_halves(x):
    half = x.shape[1] // 2
    return jnp.concatenate([x[:, :half], x[:, half:]], axis=0)


def side_halves(x):
    half = x.shape[0] // 2
    return jnp.concatenate([x[:half], x[half:]], axis=1)


def attend_tile(q, k, vt):
    factor = (HD ** -0.5) * LOG2E
    scores = dot_nt(k, q)
    top = jnp.max(scores, axis=0, keepdims=True)
    expo = jnp.exp2((scores - top) * factor)
    den = jnp.sum(expo, axis=0, keepdims=True)
    out = dot_nn(vt, expo.astype(jnp.bfloat16))
    return out / den, top * factor + jnp.log2(den)


def packed(out, lse):
    half = lse.shape[1] // 2
    rows = []
    rest = lse
    for _ in range(3):
        part = rest.astype(jnp.bfloat16).astype(jnp.float32)
        rest = rest - part
        rows += [part[:, :half], part[:, half:]]
    rows.append(jnp.zeros((STAT - 6, half), jnp.float32))
    return jnp.concatenate([stack_halves(out)] + rows, axis=0).astype(jnp.bfloat16)


def unpacked(block):
    rows = block.shape[0] - STAT
    out = side_halves(block[:rows]).astype(jnp.float32)
    stat = block[rows:].astype(jnp.float32)
    pair = [stat[i : i + 1] + stat[i + 2 : i + 3] + stat[i + 4 : i + 5] for i in range(2)]
    return out, jnp.concatenate(pair, axis=1)


def order_kernel(s, q_ref, k_ref, v_ref, qp, kp, vt, swap, near, mate, far, vp):
    heads, strides, block, _ = qp.shape
    part = block // strides
    row = lax.broadcasted_iota(jnp.int32, (block, block), 0)
    col = lax.broadcasted_iota(jnp.int32, (block, block), 1)
    pick = (col == strides * (row % part) + row // part).astype(jnp.bfloat16)
    for src, dst in ((q_ref, qp), (k_ref, kp), (v_ref, vp)):
        for b in range(strides):
            y = dot_nn(pick, src[b * block : (b + 1) * block, :]).astype(jnp.bfloat16)
            for h in range(heads):
                for j in range(strides):
                    dst[h, j, b * part : (b + 1) * part, :] = y[
                        j * part : (j + 1) * part, h * HD : (h + 1) * HD
                    ]
    er = lax.broadcasted_iota(jnp.int32, (HD, HD), 0)
    ec = lax.broadcasted_iota(jnp.int32, (HD, HD), 1)
    eye = (er == ec).astype(jnp.bfloat16)
    for h in range(heads):
        for j in range(strides):
            vt[h, j] = stack_halves(dot_nt(eye, vp[h, j]).astype(jnp.bfloat16))
    side = s[4]
    for i in range(2):
        swap[i] = kp[0, s[0] + 2 * i]
        swap[2 + i] = vt[0, s[0] + 2 * i]
        mate[i] = qp[1, s[1] + 2 * i]
        mate[2 + i] = kp[1, s[1] + 2 * i]
        mate[4 + i] = vt[1, s[1] + 2 * i]
    for dst, h in ((near, side), (far, 1 - side)):
        for i, src in enumerate((qp, kp, vt)):
            dst[i] = src[h, s[2 + h]]


def local_kernel(q_ref, k_ref, v_ref, o_ref, l_ref):
    strides, block, _ = q_ref.shape[1:]
    k = k_ref[0].reshape(strides * block, HD)
    vt = jnp.concatenate([side_halves(v_ref[0, j]) for j in range(strides)], axis=1)
    for j in range(strides):
        out, lse = attend_tile(q_ref[0, j], k, vt)
        o_ref[0, j] = out
        l_ref[0, j : j + 1, :] = lse


def full_kernel(s, qp, kp, vt, near, mate, far, other, o_ref, qs, ks, vs):
    edge = s[5]
    side = s[4]
    count, block, _ = qs.shape

    @pl.when(edge == 1)
    def _():
        for i in range(2):
            for n, (own, dst) in enumerate(((qp, qs), (kp, ks), (vt, vs))):
                dst[i] = own[1, s[1] + 2 * i]
                dst[2 + i] = mate[2 * n + i]

    @pl.when(edge == 0)
    def _():
        for n, (own, dst) in enumerate(((qp, qs), (kp, ks), (vt, vs))):
            dst[0] = own[side, s[2 + side]]
            dst[1] = near[n]
            dst[2] = far[n]
            dst[3] = other[n]

    k = ks[...].reshape(count * block, HD)
    v = jnp.concatenate([side_halves(vs[j]) for j in range(count)], axis=1)
    for j in range(count):
        o_ref[j] = packed(*attend_tile(qs[j], k, v))


def half_kernel(s, qp, kp, vt, swap, o_ref):
    k = jnp.concatenate([kp[0, s[0]], kp[0, s[0] + 2], swap[0], swap[1]], axis=0)
    v = jnp.concatenate(
        [side_halves(x) for x in (vt[0, s[0]], vt[0, s[0] + 2], swap[2], swap[3])], axis=1
    )
    for i in range(2):
        o_ref[i] = packed(*attend_tile(qp[0, s[0] + 2 * i], k, v))


def merge_kernel(s, o0, l0, half, full, mate, near, far, other, a_ref, one, two, wide):
    edge = s[5]
    side = s[4]
    heads, strides, _, block = o0.shape
    for i in range(2):
        one[0, i] = half[i]

    @pl.when(edge == 1)
    def _():
        for i in range(2):
            one[1, i] = full[i]
        two[side] = near[0]
        two[1 - side] = far[0]

    @pl.when(edge == 0)
    def _():
        for i in range(2):
            one[1, i] = mate[i]
        two[side] = full[0]
        two[1 - side] = other[0]

    for h in range(heads):
        out2, lse2 = unpacked(two[h])
        for j in range(strides):
            out1, lse1 = unpacked(one[h, j // 2])
            lse1j = jnp.where(s[h] == j % 2, lse1, NEG)
            lse2j = jnp.where(s[2 + h] == j, lse2, NEG)
            lse0 = l0[h, j : j + 1, :]
            big = jnp.maximum(lse0, jnp.maximum(lse1j, lse2j))
            w0 = jnp.exp2(lse0 - big)
            w1 = jnp.exp2(lse1j - big)
            w2 = jnp.exp2(lse2j - big)
            total = 1.0 / (w0 + w1 + w2)
            mixed = (w0 * total) * o0[h, j] + (w1 * total) * out1 + (w2 * total) * out2
            mixed = mixed.astype(jnp.bfloat16)
            for c in range(2):
                wide[c, h * HD : (h + 1) * HD, j * (block // 2) : (j + 1) * (block // 2)] = mixed[
                    :, c * (block // 2) : (c + 1) * (block // 2)
                ]
    width = wide.shape[2]
    run = width // strides
    row = lax.broadcasted_iota(jnp.int32, (width, width), 0)
    col = lax.broadcasted_iota(jnp.int32, (width, width), 1)
    back = (row == strides * (col % run) + col // run).astype(jnp.bfloat16)
    for c in range(2):
        a_ref[c * width : (c + 1) * width, :] = dot_nt(back, wide[c]).astype(jnp.bfloat16)


def project_kernel(*refs):
    *ins, o_ref = refs
    total = None
    start = 0
    if len(ins) % 2:
        total = ins[0][...]
        start = 1
    n = (len(ins) - start) // 2
    for a, w in zip(ins[start : start + n], ins[start + n :]):
        term = dot_nn(a[...], w[...])
        total = term if total is None else total + term
    o_ref[...] = total.astype(o_ref.dtype)


def cost(flops, size):
    return pl.CostEstimate(flops=flops, bytes_accessed=size, transcendentals=0)


VM = pltpu.VMEM
SMEM_SPEC = pl.BlockSpec(memory_space=pltpu.SMEM)
FULL_SPEC = pl.BlockSpec(memory_space=pltpu.VMEM)
PARAMS = pltpu.CompilerParams(vmem_limit_bytes=40 << 20)
BF = jnp.bfloat16


def fast_shards(queries, keys, values, offsets, w_out):
    rows = queries.shape[0]
    local_heads = queries.shape[1] // HD
    pairs = local_heads // 2
    width = queries.shape[1]
    strides = lax.axis_size("ctx")
    block = rows // strides
    ctx = lax.axis_index("ctx")
    head = lax.axis_index("head")
    side = ctx // 2
    edge = ((ctx == 0) | (ctx == strides - 1)).astype(jnp.int32)
    mine = lax.dynamic_slice_in_dim(offsets, head * local_heads, local_heads, axis=1)
    unit = (block, HD)
    sds = jax.ShapeDtypeStruct

    to_mid = [(0, 1), (3, 2)]
    to_edge = [(1, 0), (2, 3)]
    far_in = [(0, 2), (3, 1)]
    far_out = [(2, 0), (1, 3)]
    mids = [(1, 2), (2, 1)]
    mates = [(0, 1), (1, 0), (2, 3), (3, 2)]

    def send(x, pairs_of):
        return lax.ppermute(x, "ctx", pairs_of)

    def cross(x, bit):
        return lax.ppermute(x, "head", [(i, i ^ bit) for i in range(lax.axis_size("head"))])

    def w_block(bit):
        return lax.dynamic_slice_in_dim(w_out, (head ^ bit) * width, width, axis=1)

    scal = []
    for p in range(pairs):
        scal.append(
            jnp.concatenate(
                [mine[1, 2 * p : 2 * p + 2], mine[2, 2 * p : 2 * p + 2], jnp.stack([side, edge])]
            )
        )

    ordered = []
    sent = []
    for p in range(pairs):
        shape = (2, strides, *unit)
        res = pl.pallas_call(
            order_kernel,
            out_shape=[sds(shape, BF)] * 3
            + [sds((4, *unit), BF), sds((3, *unit), BF), sds((6, *unit), BF), sds((3, *unit), BF)],
            grid=(1,),
            in_specs=[SMEM_SPEC] + [pl.BlockSpec((rows, 2 * HD), lambda i, p=p: (0, p))] * 3,
            out_specs=[FULL_SPEC] * 7,
            scratch_shapes=[VM(shape, BF)],
            compiler_params=PARAMS,
            cost_estimate=cost(2 * 3 * rows * block * 2 * HD, 12 * rows * HD * 2),
            name="order",
        )(scal[p], queries, keys, values)
        qp, kp, vt, swap, near, mate, far = res
        ordered.append((qp, kp, vt))
        sent.append(
            (
                send(near, to_mid),
                send(mate, to_edge),
                send(far, far_in),
                send(far, mids),
                send(swap, mates),
            )
        )

    w_mine = [w_block(0)] + [cross(w_block(bit), bit) for bit in (1, 2, 3)]

    local = []
    for p in range(pairs):
        spec = pl.BlockSpec((1, strides, *unit), lambda h: (h, 0, 0, 0))
        local.append(
            pl.pallas_call(
                local_kernel,
                out_shape=[sds((2, strides, HD, block), jnp.float32), sds((2, strides, block), jnp.float32)],
                grid=(2,),
                in_specs=[spec] * 3,
                out_specs=[
                    pl.BlockSpec((1, strides, HD, block), lambda h: (h, 0, 0, 0)),
                    pl.BlockSpec((1, strides, block), lambda h: (h, 0, 0)),
                ],
                compiler_params=PARAMS,
                cost_estimate=cost(8 * rows * rows * HD, 16 * rows * HD),
                name="local",
            )(*ordered[p])
        )

    total = None
    for p in range(pairs):
        near, mate, far, other, swap = sent[p]
        full = pl.pallas_call(
            full_kernel,
            out_shape=sds((4, block + STAT, HD), BF),
            in_specs=[SMEM_SPEC] + [FULL_SPEC] * 7,
            out_specs=FULL_SPEC,
            scratch_shapes=[VM((4, *unit), BF)] * 3,
            compiler_params=PARAMS,
            cost_estimate=cost(4 * rows * rows * HD, 16 * rows * HD),
            name="full",
        )(scal[p], *ordered[p], near, mate, far, other)
        back_mate = send(full[2:4], to_mid)
        back_near = send(full[1:2], to_edge)
        back_far = send(full[2:3], far_out)
        back_other = send(full[3:4], mids)
        half = pl.pallas_call(
            half_kernel,
            out_shape=sds((2, block + STAT, HD), BF),
            in_specs=[SMEM_SPEC] + [FULL_SPEC] * 4,
            out_specs=FULL_SPEC,
            compiler_params=PARAMS,
            cost_estimate=cost(2 * rows * rows * HD, 16 * rows * HD),
            name="half",
        )(scal[p], *ordered[p], swap)
        attn = pl.pallas_call(
            merge_kernel,
            out_shape=sds((rows, 2 * HD), BF),
            in_specs=[SMEM_SPEC] + [FULL_SPEC] * 8,
            out_specs=FULL_SPEC,
            scratch_shapes=[
                VM((2, 2, block + STAT, HD), BF),
                VM((2, block + STAT, HD), BF),
                VM((2, 2 * HD, strides * (block // 2)), BF),
            ],
            compiler_params=PARAMS,
            cost_estimate=cost(4 * rows * rows * HD, 16 * rows * HD),
            name="merge",
        )(scal[p], *local[p], half, full, back_mate, back_near, back_far, back_other)
        over = cross(attn, 2)
        beside = cross(attn, 1)
        corner = cross(over, 1)
        for group, last in (
            (((attn, 0), (beside, 1)), False),
            (((over, 2), (corner, 3)), p == pairs - 1),
        ):
            tile = rows // 4
            ins = [] if total is None else [total]
            specs = [] if total is None else [pl.BlockSpec((tile, width), lambda i: (i, 0))]
            ins += [a for a, _ in group] + [w_mine[bit] for _, bit in group]
            specs += [pl.BlockSpec((tile, 2 * HD), lambda i: (i, 0))] * len(group)
            specs += [pl.BlockSpec((2 * HD, width), lambda i, p=p: (p, 0))] * len(group)
            total = pl.pallas_call(
                project_kernel,
                out_shape=sds((rows, width), BF if last else jnp.float32),
                grid=(4,),
                in_specs=specs,
                out_specs=pl.BlockSpec((tile, width), lambda i: (i, 0)),
                compiler_params=PARAMS,
                cost_estimate=cost(4 * rows * 2 * HD * width, rows * width * 4),
                name="project",
            )(*ins)
    return total


def solution(mesh):
    sizes = dict(mesh.shape)
    fast = sizes["ctx"] == 4 and sizes["head"] == 4
    return jax.shard_map(
        fast_shards if fast else shards,
        mesh=mesh,
        in_specs=(
            P(("groups", "ctx"), "head"),
            P(("groups", "ctx"), "head"),
            P(("groups", "ctx"), "head"),
            P(),
            P("head", None),
        ),
        out_specs=P(("groups", "ctx"), "head"),
        check_vma=False,
    )
```
